32 devices in a mesh: dp: 4 (over z), zero: 8 (over y, x, core).
Axes of the slice: x: 2, y: 2, z: 4, core: 2. Of those that a mesh axis runs over, the one named last changes fastest.
Arguments:
- block_input: float32 [4, 1024, 1024], P('dp', 'zero'), may hold values from -6 to 6
- out_cotangent: float32 [4, 1024, 1024], P('dp', 'zero'), may hold values from -6 to 6
- segment_ids: int32 [4, 1024], P('dp'), may hold values from 0 to 3, never falling along the last dimension, each value on 1 to 512 neighbouring positions
- query_key_value_weight: float32 [1024, 4096], P(('dp', 'zero')), may hold values from -0.1875 to 0.1875
- w_out: float32 [2048, 1024], P(('dp', 'zero')), may hold values from -1 to 1
- w_gateup: float32 [1024, 6144], P(('dp', 'zero')), may hold values from -0.1875 to 0.1875
- w_down: float32 [3072, 1024], P(('dp', 'zero')), may hold values from -0.109375 to 0.109375
- norm_gains: float32 [1024, 2], P(('dp', 'zero')), may hold values from 0.5 to 1.5
- head_gains: float32 [128, 2], P(('dp', 'zero')), may hold values from 0.5 to 2.4, as said below
- first_moment_projection: float32 [1024, 4096], P(('dp', 'zero')), may hold values from -96 to 96
- mean_out: float32 [2048, 1024], P(('dp', 'zero')), may hold values from -19.2 to 19.2
- mean_gateup: float32 [1024, 6144], P(('dp', 'zero')), may hold values from -19.2 to 19.2
- mean_down: float32 [3072, 1024], P(('dp', 'zero')), may hold values from -19.2 to 19.2
- mean_norms: float32 [1024, 2], P(('dp', 'zero')), may hold values from -153.6 to 153.6
- mean_heads: float32 [128, 2], P(('dp', 'zero')), may hold values from -96 to 96
- second_moment_projection: float32 [1024, 4096], P(('dp', 'zero')), may hold values from 245.76 to 2457.6
- square_out: float32 [2048, 1024], P(('dp', 'zero')), may hold values from 8.192 to 81.92
- square_gateup: float32 [1024, 6144], P(('dp', 'zero')), may hold values from 8.192 to 81.92
- square_down: float32 [3072, 1024], P(('dp', 'zero')), may hold values from 8.192 to 81.92
- square_norms: float32 [1024, 2], P(('dp', 'zero')), may hold values from 409.6 to 4096
- square_heads: float32 [128, 2], P(('dp', 'zero')), may hold values from 204.8 to 2048
Outputs:
- block_output: float32 [4, 1024, 1024], P('dp', 'zero')
- input_grad: float32 [4, 1024, 1024], P('dp', 'zero')
- grad_qkv: float32 [1024, 4096], P(('dp', 'zero'))
- grad_out: float32 [2048, 1024], P(('dp', 'zero'))
- grad_gateup: float32 [1024, 6144], P(('dp', 'zero'))
- grad_down: float32 [3072, 1024], P(('dp', 'zero'))
- grad_norms: float32 [1024, 2], P(('dp', 'zero'))
- grad_heads: float32 [128, 2], P(('dp', 'zero'))
- next_qkv: float32 [1024, 4096], P(('dp', 'zero'))
- next_out: float32 [2048, 1024], P(('dp', 'zero'))
- next_gateup: float32 [1024, 6144], P(('dp', 'zero'))
- next_down: float32 [3072, 1024], P(('dp', 'zero'))
- next_norms: float32 [1024, 2], P(('dp', 'zero'))
- next_heads: float32 [128, 2], P(('dp', 'zero'))
- next_mean_qkv: float32 [1024, 4096], P(('dp', 'zero'))
- next_mean_out: float32 [2048, 1024], P(('dp', 'zero'))
- next_mean_gateup: float32 [1024, 6144], P(('dp', 'zero'))
- next_mean_down: float32 [3072, 1024], P(('dp', 'zero'))
- next_mean_norms: float32 [1024, 2], P(('dp', 'zero'))
- next_mean_heads: float32 [128, 2], P(('dp', 'zero'))
- next_square_qkv: float32 [1024, 4096], P(('dp', 'zero'))
- next_square_out: float32 [2048, 1024], P(('dp', 'zero'))
- next_square_gateup: float32 [1024, 6144], P(('dp', 'zero'))
- next_square_down: float32 [3072, 1024], P(('dp', 'zero'))
- next_square_norms: float32 [1024, 2], P(('dp', 'zero'))
- next_square_heads: float32 [128, 2], P(('dp', 'zero'))
The draws below stay inside these ranges and needn't reach their ends.
Inputs may be any that keep to these rules, and one draw needn't show every extreme that they name: `segment_ids`: along each sequence the number never falls; each of the 4 documents has 1 to 512 tokens, one exactly 512. `head_gains`: positive gains.
All inputs are finite; a program needn't handle non-finite values.
Results may differ from the reference program's by a relative error of at most 0.04.
Values may be sent and summed in bfloat16 or wider, within the bound.
No kernel may reach another device: no remote copies, remote signals or barrier semaphores. Data moves between devices by JAX's collectives and lax.ppermute only.
A program may use at most 192 MiB of HBM per device.

```python
import math
import jax
import jax.numpy as jnp
import numpy as np
from jax import lax

MODEL_WIDTH = 1024
QUERY_HEADS = 16
KEY_VALUE_HEADS = 8
HEAD_SIZE = 128
FF = 3072
DOCS = 4
SEQ = 1024
SEQS = 4


def draw_head_gains(key, part):
    values = jax.random.uniform(key, (HEAD_SIZE, 2), jnp.float32, 0.5, 1.6)
    return values


def with_spikes(array, own_key, source, target, blocks, factor):
    owner, partner = [(jnp.arange(array.shape[position]) // (array.shape[position] // blocks)).reshape([-1 if axis == position else 1 for axis in range(array.ndim)]) for position in (source, target)]
    chosen = jax.random.permutation(own_key, blocks)[partner]
    strong = (owner == chosen) | (owner == (partner + blocks // 2) % blocks)
    return jnp.where(strong, factor * array, array)


def shard_levels(stream_key, extent, cuts, smallest, high):
    def one(dim, blocks):
        heights = jax.random.uniform(jax.random.fold_in(jax.random.fold_in(stream_key, 6), dim), (blocks,), jnp.float32, smallest / len(cuts), high / len(cuts))
        return jnp.repeat(jnp.exp(heights), extent[dim] // blocks).reshape((-1,) + (1,) * (len(extent) - dim - 1))

    factor_of = one(*cuts[0])
    for cut in cuts[1:]:
        factor_of = factor_of * one(*cut)
    return factor_of


def length_profile(count, total, reach, lean):
    loads = [(1 << 20) // math.isqrt(standing ** lean) + 1 for standing in range(2, count + 1)]
    surplus, holding = total - reach - (count - 1), [1] * (count - 1)
    while surplus > 0:
        movable = [i for i in range(count - 1) if holding[i] < reach]
        pool, left = sum([loads[i] for i in movable]), surplus
        for i in movable:
            more = min(reach - holding[i], max(1, left * loads[i] // pool), surplus)
            holding[i] = holding[i] + more
            surplus = surplus - more
    return np.array([reach] + holding)


def uneven(key, number_of, total, limit, skew):
    if number_of == 2:
        one = jax.random.randint(key, (), max(1, total - limit), min(limit, total - 1) + 1)
        return jnp.stack([one, total - one])
    sizes = jnp.asarray(length_profile(number_of, total, limit, skew), jnp.int32)
    twos = (number_of - 1) // 2
    donor, receiver = sizes[1:1 + 2 * twos:2], sizes[2:2 + 2 * twos:2]
    margin = jnp.minimum(donor - 1, limit - receiver)
    shifted = jax.random.randint(jax.random.fold_in(key, 1), (twos,), 0, 1 << 20) % (margin + 1)
    sizes = sizes.at[1:1 + 2 * twos:2].set(donor - shifted).at[2:2 + 2 * twos:2].set(receiver + shifted)
    return sizes[jax.random.permutation(jax.random.fold_in(key, 2), number_of)]


def noise(own_key, shape, spread, most, pieces=(), held_as=jnp.bfloat16):
    entries = spread * jax.random.normal(own_key, shape, jnp.float32)
    if pieces:
        entries = entries * shard_levels(own_key, shape, pieces, -0.22, 0.18)
    return jnp.clip(entries, -most, most).astype(held_as)


def bell_draw_with(key, extent, scale, reach, split, heavy, kind=jnp.bfloat16):
    drawn = scale * jax.random.normal(key, extent, jnp.float32)
    if split:
        drawn = drawn * shard_levels(key, extent, split, -0.22, 0.18)
    return jnp.clip(with_spikes(drawn, jax.random.fold_in(key, 3), *heavy), -reach, reach).astype(kind)


def setup_inputs(seed: int = 0) -> dict:
    streams_of = jax.random.split(jax.random.key(seed), 22)
    return {
        "block_input": bell_draw_with(streams_of[0], (SEQS, SEQ, MODEL_WIDTH), 1.0, 6.0, ((0, 4), (1, 8)), (1, 2, 8, 2.0), jnp.float32),
        "out_cotangent": noise(streams_of[1], (SEQS, SEQ, MODEL_WIDTH), 1.0, 6.0, ((0, 4), (1, 8)), jnp.float32),
        "segment_ids": jax.vmap(lambda own: jnp.searchsorted(jnp.cumsum(uneven(own, DOCS, SEQ, SEQ // 2, 0)), jnp.arange(SEQ), side="right"))(jax.random.split(streams_of[2], SEQS)).reshape((SEQS, SEQ)).astype(jnp.int32),
        "query_key_value_weight": noise(streams_of[3], (MODEL_WIDTH, (QUERY_HEADS + 2 * KEY_VALUE_HEADS) * HEAD_SIZE), MODEL_WIDTH ** -0.5, 0.1875, ((0, 32),), jnp.float32),
        "w_out": noise(streams_of[4], (QUERY_HEADS * HEAD_SIZE, MODEL_WIDTH), (QUERY_HEADS * HEAD_SIZE // 64) ** -0.5, 1.0, ((0, 32),), jnp.float32),
        "w_gateup": noise(streams_of[5], (MODEL_WIDTH, 2 * FF), MODEL_WIDTH ** -0.5, 0.1875, ((0, 32),), jnp.float32),
        "w_down": noise(streams_of[6], (FF, MODEL_WIDTH), FF ** -0.5, 0.109375, ((0, 32),), jnp.float32),
        "norm_gains": jnp.clip(1.0 + 0.1 * jax.random.normal(streams_of[7], (MODEL_WIDTH, 2), jnp.float32), 0.5, 1.5),
        "head_gains": draw_head_gains(jax.random.fold_in(streams_of[21], 71), 0),
        "first_moment_projection": noise(streams_of[9], (MODEL_WIDTH, (QUERY_HEADS + 2 * KEY_VALUE_HEADS) * HEAD_SIZE), (0.25 * (SEQS * SEQ) ** 0.5), 96.0, ((0, 32),), jnp.float32),
        "mean_out": noise(streams_of[10], (QUERY_HEADS * HEAD_SIZE, MODEL_WIDTH), (0.05 * (SEQS * SEQ) ** 0.5), 19.2, ((0, 32),), jnp.float32),
        "mean_gateup": noise(streams_of[11], (MODEL_WIDTH, 2 * FF), (0.05 * (SEQS * SEQ) ** 0.5), 19.2, ((0, 32),), jnp.float32),
        "mean_down": noise(streams_of[12], (FF, MODEL_WIDTH), (0.05 * (SEQS * SEQ) ** 0.5), 19.2, ((0, 32),), jnp.float32),
        "mean_norms": noise(streams_of[13], (MODEL_WIDTH, 2), (0.4 * (SEQS * SEQ) ** 0.5), 153.6, ((0, 32),), jnp.float32),
        "mean_heads": noise(streams_of[14], (HEAD_SIZE, 2), (0.25 * (SEQS * SEQ) ** 0.5), 96.0, ((0, 32),), jnp.float32),
        "second_moment_projection": jnp.clip(jnp.exp(math.log(2457.6) - 2.3025852 * jax.random.uniform(streams_of[15], (MODEL_WIDTH, (QUERY_HEADS + 2 * KEY_VALUE_HEADS) * HEAD_SIZE), jnp.float32) ** shard_levels(streams_of[15], (MODEL_WIDTH, (QUERY_HEADS + 2 * KEY_VALUE_HEADS) * HEAD_SIZE), ((0, 32),), -0.2, 0.2)), 245.76, 2457.6),
        "square_out": jnp.clip(jnp.exp(math.log(81.92) - 2.30258502 * jax.random.uniform(streams_of[16], (QUERY_HEADS * HEAD_SIZE, MODEL_WIDTH), jnp.float32) ** shard_levels(streams_of[16], (QUERY_HEADS * HEAD_SIZE, MODEL_WIDTH), ((0, 32),), -0.2, 0.2)), 8.192, 81.92),
        "square_gateup": jnp.clip(jnp.exp(math.log(81.92) - 2.30258502 * jax.random.uniform(streams_of[17], (MODEL_WIDTH, 2 * FF), jnp.float32) ** shard_levels(streams_of[17], (MODEL_WIDTH, 2 * FF), ((0, 32),), -0.2, 0.2)), 8.192, 81.92),
        "square_down": jnp.clip(jnp.exp(math.log(81.92) - 2.30258502 * jax.random.uniform(streams_of[18], (FF, MODEL_WIDTH), jnp.float32) ** shard_levels(streams_of[18], (FF, MODEL_WIDTH), ((0, 32),), -0.2, 0.2)), 8.192, 81.92),
        "square_norms": jnp.clip(jnp.exp(math.log(4096.0) - 2.3025851 * jax.random.uniform(streams_of[19], (MODEL_WIDTH, 2), jnp.float32) ** shard_levels(streams_of[19], (MODEL_WIDTH, 2), ((0, 32),), -0.2, 0.2)), 409.6, 4096.0),
        "square_heads": jnp.clip(jnp.exp(math.log(2048.0) - 2.3025851 * jax.random.uniform(streams_of[20], (HEAD_SIZE, 2), jnp.float32) ** shard_levels(streams_of[20], (HEAD_SIZE, 2), ((0, 32),), -0.2, 0.2)), 204.8, 2048.0),
    }


norm_eps = 1e-06
rope_base = 1000000.0
beta_one = 0.9
beta_two = 0.95
adam_eps = 1e-08
learn_rate = 0.01
decay_rate = 0.1
step_count = 3
score_masked = -1e+30

def rotate_half(value):
    half = value.shape[-1] // 2
    return jnp.concatenate([-value[..., half:], value[..., :half]], axis=-1)

def rotate_back(value):
    half = value.shape[-1] // 2
    return jnp.concatenate([value[..., half:], -value[..., :half]], axis=-1)

def rope_tables(positions, width):
    steps_half = jnp.arange(width // 2, dtype=jnp.float32)
    frequency = rope_base ** (-(steps_half * 2.0 / width))
    angles = positions.astype(jnp.float32)[:, None] * frequency[None, :]
    angles = jnp.concatenate([angles, angles], axis=-1)
    return (jnp.cos(angles), jnp.sin(angles))

def rms_scale(value):
    return lax.rsqrt(lax.optimization_barrier(jnp.mean(value * value, axis=-1, keepdims=True)) + norm_eps)

def rms_back(grad_scaled, value, scale):
    normed = value * scale
    return scale * (grad_scaled - normed * lax.optimization_barrier(jnp.mean(grad_scaled * normed, axis=-1, keepdims=True)))

def adam_update(weight, grad, first, second):
    first_new = beta_one * first + (1.0 - beta_one) * grad
    second_new = beta_two * second + (1.0 - beta_two) * grad * grad
    first_hat = first_new / (1.0 - beta_one ** step_count)
    second_hat = second_new / (1.0 - beta_two ** step_count)
    weight_new = weight - learn_rate * (first_hat / (jnp.sqrt(second_hat) + adam_eps) + decay_rate * weight)
    return (weight_new, first_new, second_new)

def lower_precision(value):
    return lax.optimization_barrier(value.astype(jnp.bfloat16))

def sequence_pass(weights, inputs, cotangent, segments):
    qkv_weight, out_weight, gateup_weight, down_weight, gains, heads = weights
    sequence_length = inputs.shape[0]
    head_group = QUERY_HEADS // KEY_VALUE_HEADS
    query_span_width = QUERY_HEADS * HEAD_SIZE
    key_span_width = KEY_VALUE_HEADS * HEAD_SIZE
    score_scale = HEAD_SIZE ** (-0.5)
    gain_one = gains[:, 0].astype(jnp.float32)
    gain_two = gains[:, 1].astype(jnp.float32)
    query_gain = heads[:, 0].astype(jnp.float32)
    key_gain = heads[:, 1].astype(jnp.float32)
    positions = jnp.arange(sequence_length, dtype=jnp.int32)
    cosine, sine = rope_tables(positions, HEAD_SIZE)
    cosine = cosine[:, None, :]
    sine = sine[:, None, :]
    scale_one = rms_scale(inputs)
    normed_input = (inputs * scale_one * gain_one).astype(jnp.bfloat16)
    projected_output = jnp.dot(normed_input, qkv_weight, preferred_element_type=jnp.float32)
    query = projected_output[:, :query_span_width].reshape(sequence_length, QUERY_HEADS, HEAD_SIZE)
    key = projected_output[:, query_span_width:query_span_width + key_span_width].reshape(sequence_length, KEY_VALUE_HEADS, HEAD_SIZE)
    values_lower_precision = lower_precision(projected_output[:, query_span_width + key_span_width:]).reshape(sequence_length, KEY_VALUE_HEADS, HEAD_SIZE)
    query_scale = rms_scale(query)
    key_scale = rms_scale(key)
    query_normed = query * query_scale * query_gain
    key_normed = key * key_scale * key_gain
    rotated_queries = lower_precision(query_normed * cosine + rotate_half(query_normed) * sine)
    key_turned = lower_precision(key_normed * cosine + rotate_half(key_normed) * sine)
    wide_queries = rotated_queries.astype(jnp.float32).reshape(sequence_length, KEY_VALUE_HEADS, head_group, HEAD_SIZE)
    key_wide = key_turned.astype(jnp.float32)
    value_wide = values_lower_precision.astype(jnp.float32)
    allowed = (segments[:, None] == segments[None, :]) & (positions[:, None] >= positions[None, :])
    scores = jnp.einsum('tgrd,kgd->grtk', wide_queries, key_wide) * score_scale
    scores = jnp.where(allowed, scores, score_masked)
    top = lax.optimization_barrier(jnp.max(scores, axis=-1, keepdims=True))
    log_total = top + jnp.log(lax.optimization_barrier(jnp.sum(jnp.exp(scores - top), axis=-1, keepdims=True)))
    soft_weights = jnp.where(allowed, jnp.exp(scores - log_total), 0.0)
    soft_low = lower_precision(soft_weights).astype(jnp.float32)
    attention_output = lower_precision(jnp.einsum('grtk,kgd->tgrd', soft_low, value_wide)).reshape(sequence_length, query_span_width)
    middle = inputs + jnp.dot(attention_output, out_weight, preferred_element_type=jnp.float32)
    scale_two = rms_scale(middle)
    normed_mid = (middle * scale_two * gain_two).astype(jnp.bfloat16)
    gateup = jnp.dot(normed_mid, gateup_weight, preferred_element_type=jnp.float32)
    gate = gateup[:, :FF]
    upward = gateup[:, FF:]
    sigma = jax.nn.sigmoid(gate)
    hidden = (gate * sigma * upward).astype(jnp.bfloat16)
    output = middle + jnp.dot(hidden, down_weight, preferred_element_type=jnp.float32)
    cot_low = cotangent.astype(jnp.bfloat16)
    grad_down = jnp.dot(hidden.T, cot_low, preferred_element_type=jnp.float32)
    grad_hidden = jnp.dot(cot_low, down_weight.T, preferred_element_type=jnp.float32)
    gate_term = grad_hidden * upward * sigma * (1.0 + gate * (1.0 - sigma))
    up_term = grad_hidden * gate * sigma
    gateup_grad = jnp.concatenate([gate_term, up_term], axis=-1).astype(jnp.bfloat16)
    grad_gateup = jnp.dot(normed_mid.T, gateup_grad, preferred_element_type=jnp.float32)
    grad_normed_mid = jnp.dot(gateup_grad, gateup_weight.T, preferred_element_type=jnp.float32)
    grad_gain_two = lax.optimization_barrier(jnp.sum(grad_normed_mid * middle * scale_two, axis=0))
    grad_middle = cotangent + rms_back(grad_normed_mid * gain_two, middle, scale_two)
    middle_low = grad_middle.astype(jnp.bfloat16)
    grad_out = jnp.dot(attention_output.T, middle_low, preferred_element_type=jnp.float32)
    attention_output_gradient = lower_precision(jnp.dot(middle_low, out_weight.T, preferred_element_type=jnp.float32))
    wide_gradient = attention_output_gradient.astype(jnp.float32).reshape(sequence_length, KEY_VALUE_HEADS, head_group, HEAD_SIZE)
    wide_attention_output = attention_output.astype(jnp.float32).reshape(sequence_length, KEY_VALUE_HEADS, head_group, HEAD_SIZE)
    output_difference = jnp.einsum('mhln,mhln->hlm', wide_gradient, wide_attention_output)
    grad_soft = jnp.einsum('tgrd,kgd->grtk', wide_gradient, value_wide)
    grad_scores = lower_precision(soft_weights * (grad_soft - output_difference[..., None])).astype(jnp.float32)
    grad_query = jnp.einsum('grtk,kgd->tgrd', grad_scores, key_wide) * score_scale
    key_gradient = jnp.einsum('grtk,tgrd->kgd', grad_scores, wide_queries) * score_scale
    grad_value = jnp.einsum('grtk,tgrd->kgd', soft_low, wide_gradient)
    grad_query = grad_query.reshape(sequence_length, QUERY_HEADS, HEAD_SIZE)
    grad_query_normed = grad_query * cosine + rotate_back(grad_query * sine)
    grad_key_normed = key_gradient * cosine + rotate_back(key_gradient * sine)
    grad_query_gain = lax.optimization_barrier(jnp.sum(grad_query_normed * query * query_scale, axis=(0, 1)))
    grad_key_gain = lax.optimization_barrier(jnp.sum(grad_key_normed * key * key_scale, axis=(0, 1)))
    grad_query_pre = rms_back(grad_query_normed * query_gain, query, query_scale)
    grad_key_pre = rms_back(grad_key_normed * key_gain, key, key_scale)
    grad_projected = jnp.concatenate([grad_query_pre.reshape(sequence_length, query_span_width), grad_key_pre.reshape(sequence_length, key_span_width), grad_value.reshape(sequence_length, key_span_width)], axis=-1).astype(jnp.bfloat16)
    grad_qkv = jnp.dot(normed_input.T, grad_projected, preferred_element_type=jnp.float32)
    grad_normed_input = jnp.dot(grad_projected, qkv_weight.T, preferred_element_type=jnp.float32)
    grad_gain_one = lax.optimization_barrier(jnp.sum(grad_normed_input * inputs * scale_one, axis=0))
    grad_input = grad_middle + rms_back(grad_normed_input * gain_one, inputs, scale_one)
    grad_norms = jnp.stack([grad_gain_one, grad_gain_two], axis=1)
    grad_heads = jnp.stack([grad_query_gain, grad_key_gain], axis=1)
    return (output, grad_input, (grad_qkv, grad_out, grad_gateup, grad_down, grad_norms, grad_heads))

def reference(block_input, out_cotangent, segment_ids, query_key_value_weight, w_out, w_gateup, w_down, norm_gains, head_gains, first_moment_projection, mean_out, mean_gateup, mean_down, mean_norms, mean_heads, second_moment_projection, square_out, square_gateup, square_down, square_norms, square_heads):
    masters = (query_key_value_weight, w_out, w_gateup, w_down, norm_gains, head_gains)
    means = (first_moment_projection, mean_out, mean_gateup, mean_down, mean_norms, mean_heads)
    squares = (second_moment_projection, square_out, square_gateup, square_down, square_norms, square_heads)
    weights = tuple((master.astype(jnp.bfloat16) for master in masters))

    def one_sequence(totals, items):
        inputs, cotangent, segments = items
        output, grad_input, grads = sequence_pass(weights, inputs, cotangent, segments)
        totals = tuple((total + grad for total, grad in zip(totals, grads)))
        return (totals, (output, grad_input))
    start_totals = tuple((jnp.zeros(master.shape, jnp.float32) for master in masters))
    totals, (outputs, input_grads) = lax.scan(one_sequence, start_totals, (block_input, out_cotangent, segment_ids))
    updated = [adam_update(masters[index], totals[index], means[index], squares[index]) for index in range(6)]
    return (outputs, input_grads, totals[0], totals[1], totals[2], totals[3], totals[4], totals[5], updated[0][0], updated[1][0], updated[2][0], updated[3][0], updated[4][0], updated[5][0], updated[0][1], updated[1][1], updated[2][1], updated[3][1], updated[4][1], updated[5][1], updated[0][2], updated[1][2], updated[2][2], updated[3][2], updated[4][2], updated[5][2])
```

```python
import jax
import jax.numpy as jnp
from jax import lax
from jax.sharding import PartitionSpec as P

QUERY_HEADS = 16
KEY_VALUE_HEADS = 8
HEAD_SIZE = 128
FF = 3072


norm_eps = 1e-06
rope_base = 1000000.0
beta_one = 0.9
beta_two = 0.95
adam_eps = 1e-08
learn_rate = 0.01
decay_rate = 0.1
step_count = 3
score_masked = -1e30


def rotate_half(value):
    half = value.shape[-1] // 2
    return jnp.concatenate([-value[..., half:], value[..., :half]], axis=-1)


def rotate_back(value):
    half = value.shape[-1] // 2
    return jnp.concatenate([value[..., half:], -value[..., :half]], axis=-1)


def rope_tables(positions, width):
    steps_half = jnp.arange(width // 2, dtype=jnp.float32)
    frequency = rope_base ** (-(steps_half * 2.0 / width))
    angles = positions.astype(jnp.float32)[:, None] * frequency[None, :]
    angles = jnp.concatenate([angles, angles], axis=-1)
    return (jnp.cos(angles), jnp.sin(angles))


def rms_scale(value):
    return lax.rsqrt(jnp.mean(value * value, axis=-1, keepdims=True) + norm_eps)


def rms_back(grad_scaled, value, scale):
    normed = value * scale
    return scale * (grad_scaled - normed * jnp.mean(grad_scaled * normed, axis=-1, keepdims=True))


def adam_update(weight, grad, first, second):
    first_new = beta_one * first + (1.0 - beta_one) * grad
    second_new = beta_two * second + (1.0 - beta_two) * grad * grad
    first_hat = first_new / (1.0 - beta_one**step_count)
    second_hat = second_new / (1.0 - beta_two**step_count)
    weight_new = weight - learn_rate * (
        first_hat / (jnp.sqrt(second_hat) + adam_eps) + decay_rate * weight
    )
    return (weight_new, first_new, second_new)


def on_device_gathered(
    block_input,
    out_cotangent,
    segment_ids,
    query_key_value_weight,
    w_out,
    w_gateup,
    w_down,
    norm_gains,
    head_gains,
    first_moment_projection,
    mean_out,
    mean_gateup,
    mean_down,
    mean_norms,
    mean_heads,
    second_moment_projection,
    square_out,
    square_gateup,
    square_down,
    square_norms,
    square_heads,
):
    masters = (query_key_value_weight, w_out, w_gateup, w_down, norm_gains, head_gains)
    means = (first_moment_projection, mean_out, mean_gateup, mean_down, mean_norms, mean_heads)
    squares = (
        second_moment_projection,
        square_out,
        square_gateup,
        square_down,
        square_norms,
        square_heads,
    )
    low_qkv = query_key_value_weight.astype(jnp.bfloat16)
    low_out = w_out.astype(jnp.bfloat16)
    low_gateup = w_gateup.astype(jnp.bfloat16)
    low_down = w_down.astype(jnp.bfloat16)
    low_norms = norm_gains.astype(jnp.bfloat16)
    low_heads = head_gains.astype(jnp.bfloat16)
    collected = (
        lax.all_gather(low_qkv, ("dp", "zero"), axis=0, tiled=True),
        lax.all_gather(low_out, ("dp", "zero"), axis=0, tiled=True),
        lax.all_gather(low_gateup, ("dp", "zero"), axis=0, tiled=True),
        lax.all_gather(low_down, ("dp", "zero"), axis=0, tiled=True),
        lax.all_gather(low_norms, ("dp", "zero"), axis=0, tiled=True),
        lax.all_gather(low_heads, ("dp", "zero"), axis=0, tiled=True),
    )
    qkv_weight, out_weight, gateup_weight, down_weight, gains, heads = collected
    inputs = block_input[0]
    cotangent = out_cotangent[0]
    segments = segment_ids[0]
    token_rows = inputs.shape[0]
    sequence_length = segments.shape[0]
    head_group = QUERY_HEADS // KEY_VALUE_HEADS
    query_span_width = QUERY_HEADS * HEAD_SIZE
    key_span_width = KEY_VALUE_HEADS * HEAD_SIZE
    score_scale = HEAD_SIZE ** (-0.5)
    first_row = lax.axis_index("zero") * token_rows
    last_row = first_row + token_rows - 1
    positions = first_row + jnp.arange(token_rows, dtype=jnp.int32)
    query_segments = lax.dynamic_slice_in_dim(segments, first_row, token_rows)
    cosine, sine = rope_tables(positions, HEAD_SIZE)
    cosine = cosine[:, None, :]
    sine = sine[:, None, :]
    gain_one = gains[:, 0].astype(jnp.float32)
    gain_two = gains[:, 1].astype(jnp.float32)
    query_gain = heads[:, 0].astype(jnp.float32)
    key_gain = heads[:, 1].astype(jnp.float32)
    scale_one = rms_scale(inputs)
    normed_input = (inputs * scale_one * gain_one).astype(jnp.bfloat16)
    projected_output = jnp.dot(normed_input, qkv_weight, preferred_element_type=jnp.float32)
    query = projected_output[:, :query_span_width].reshape(token_rows, QUERY_HEADS, HEAD_SIZE)
    key = projected_output[:, query_span_width : query_span_width + key_span_width].reshape(
        token_rows, KEY_VALUE_HEADS, HEAD_SIZE
    )
    value_local = projected_output[:, query_span_width + key_span_width :].astype(jnp.bfloat16)
    query_scale = rms_scale(query)
    key_scale = rms_scale(key)
    query_normed = query * query_scale * query_gain
    key_normed = key * key_scale * key_gain
    rotated_queries = (query_normed * cosine + rotate_half(query_normed) * sine).astype(
        jnp.bfloat16
    )
    key_turned = (
        (key_normed * cosine + rotate_half(key_normed) * sine)
        .astype(jnp.bfloat16)
        .reshape(token_rows, key_span_width)
    )
    grouped_queries = rotated_queries.reshape(token_rows, KEY_VALUE_HEADS, head_group, HEAD_SIZE)

    def block_mask(key_start, running_count):
        key_positions = key_start + jnp.arange(running_count, dtype=jnp.int32)
        key_segments = lax.dynamic_slice_in_dim(segments, key_start, running_count)
        same_doc = query_segments[:, None] == key_segments[None, :]
        return same_doc & (positions[:, None] >= key_positions[None, :])

    initial = (
        jnp.full((KEY_VALUE_HEADS, head_group, token_rows), score_masked, jnp.float32),
        jnp.zeros((KEY_VALUE_HEADS, head_group, token_rows), jnp.float32),
        jnp.zeros((KEY_VALUE_HEADS, head_group, token_rows, HEAD_SIZE), jnp.float32),
    )
    block_number = min(512, sequence_length)
    block_count = sequence_length // block_number
    block_keys = lax.all_gather(key_turned, "zero", axis=0, tiled=True)
    block_values = lax.all_gather(value_local, "zero", axis=0, tiled=True)
    key_start = jnp.int32(0)
    running_count = block_keys.shape[0]

    def attend_live(carried):
        top, total, accum = carried
        keys_threefold = block_keys.reshape(running_count, KEY_VALUE_HEADS, HEAD_SIZE)
        values_threefold = block_values.reshape(running_count, KEY_VALUE_HEADS, HEAD_SIZE)
        allowed = block_mask(key_start, running_count)
        scores = (
            jnp.einsum(
                "tgrd,kgd->grtk",
                grouped_queries,
                keys_threefold,
                preferred_element_type=jnp.float32,
            )
            * score_scale
        )
        scores = jnp.where(allowed, scores, score_masked)
        new_top = jnp.maximum(top, jnp.max(scores, axis=-1))
        weights = jnp.where(allowed, jnp.exp(scores - new_top[..., None]), 0.0)
        new_total = jnp.sum(weights, axis=-1)
        added = jnp.einsum(
            "grtk,kgd->grtd",
            weights.astype(jnp.bfloat16),
            values_threefold,
            preferred_element_type=jnp.float32,
        )
        return (new_top, new_total, added)

    top, total, accum = lax.cond(
        key_start <= last_row, attend_live, lambda carried: carried, initial
    )
    every_key, every_value = (
        lax.all_gather(key_turned, "zero", axis=0, tiled=True),
        lax.all_gather(value_local, "zero", axis=0, tiled=True),
    )
    log_total = top + jnp.log(total)
    attention_output = (
        jnp.transpose(accum / total[..., None], (2, 0, 1, 3))
        .reshape(token_rows, query_span_width)
        .astype(jnp.bfloat16)
    )
    middle = inputs + jnp.dot(attention_output, out_weight, preferred_element_type=jnp.float32)
    scale_two = rms_scale(middle)
    normed_mid = (middle * scale_two * gain_two).astype(jnp.bfloat16)
    gateup = jnp.dot(normed_mid, gateup_weight, preferred_element_type=jnp.float32)
    gate = gateup[:, :FF]
    upward = gateup[:, FF:]
    sigma = jax.nn.sigmoid(gate)
    hidden = (gate * sigma * upward).astype(jnp.bfloat16)
    output = middle + jnp.dot(hidden, down_weight, preferred_element_type=jnp.float32)
    cot_low = cotangent.astype(jnp.bfloat16)
    grad_down = jnp.einsum("tf,td->fd", hidden, cot_low, preferred_element_type=jnp.float32)
    grad_hidden = jnp.einsum("td,fd->tf", cot_low, down_weight, preferred_element_type=jnp.float32)
    gate_term = grad_hidden * upward * sigma * (1.0 + gate * (1.0 - sigma))
    up_term = grad_hidden * gate * sigma
    gateup_grad = jnp.concatenate([gate_term, up_term], axis=-1).astype(jnp.bfloat16)
    grad_gateup = jnp.einsum(
        "td,tf->df", normed_mid, gateup_grad, preferred_element_type=jnp.float32
    )
    grad_normed_mid = jnp.einsum(
        "tf,df->td", gateup_grad, gateup_weight, preferred_element_type=jnp.float32
    )
    grad_gain_two = jnp.sum(grad_normed_mid * middle * scale_two, axis=0)
    grad_middle = cotangent + rms_back(grad_normed_mid * gain_two, middle, scale_two)
    middle_low = grad_middle.astype(jnp.bfloat16)
    grad_out = jnp.einsum(
        "tq,td->qd", attention_output, middle_low, preferred_element_type=jnp.float32
    )
    attention_output_gradient = jnp.einsum(
        "td,qd->tq", middle_low, out_weight, preferred_element_type=jnp.float32
    ).astype(jnp.bfloat16)
    grouped_gradient = attention_output_gradient.reshape(
        token_rows, KEY_VALUE_HEADS, head_group, HEAD_SIZE
    )
    grouped_attention_output = attention_output.reshape(
        token_rows, KEY_VALUE_HEADS, head_group, HEAD_SIZE
    )
    output_difference = jnp.einsum(
        "mhln,mhln->hlm",
        grouped_gradient,
        grouped_attention_output,
        preferred_element_type=jnp.float32,
    )

    def back_block(grad_query, index):
        start_offset = index * block_number
        block_keys = lax.dynamic_slice_in_dim(every_key, start_offset, block_number).reshape(
            block_number, KEY_VALUE_HEADS, HEAD_SIZE
        )
        block_values = lax.dynamic_slice_in_dim(every_value, start_offset, block_number).reshape(
            block_number, KEY_VALUE_HEADS, HEAD_SIZE
        )

        def back_live(carried):
            allowed = block_mask(start_offset, block_number)
            scores = (
                jnp.einsum(
                    "tgrd,kgd->grtk",
                    grouped_queries,
                    block_keys,
                    preferred_element_type=jnp.float32,
                )
                * score_scale
            )
            soft = jnp.where(allowed, jnp.exp(scores - log_total[..., None]), 0.0)
            soft_low = soft.astype(jnp.bfloat16)
            value_term = jnp.einsum(
                "grtk,tgrd->kgd", soft_low, grouped_gradient, preferred_element_type=jnp.float32
            )
            grad_soft = jnp.einsum(
                "tgrd,kgd->grtk", grouped_gradient, block_values, preferred_element_type=jnp.float32
            )
            grad_scores = (soft * (grad_soft - output_difference[..., None])).astype(jnp.bfloat16)
            new_query = carried + jnp.einsum(
                "grtk,kgd->tgrd", grad_scores, block_keys, preferred_element_type=jnp.float32
            )
            key_term = (
                jnp.einsum(
                    "grtk,tgrd->kgd",
                    grad_scores,
                    grouped_queries,
                    preferred_element_type=jnp.float32,
                )
                * score_scale
            )
            return (
                new_query,
                key_term.reshape(block_number, key_span_width),
                value_term.reshape(block_number, key_span_width),
            )

        def skipped(carried):
            empty = jnp.zeros((block_number, key_span_width), jnp.float32)
            return (carried, empty, empty)

        new_query, key_term, value_term = lax.cond(
            start_offset <= last_row, back_live, skipped, grad_query
        )
        return (new_query, (key_term, value_term))

    grad_query, (key_terms, value_terms) = lax.scan(
        back_block,
        jnp.zeros((token_rows, KEY_VALUE_HEADS, head_group, HEAD_SIZE), jnp.float32),
        jnp.arange(block_count, dtype=jnp.int32),
    )
    key_terms = key_terms.reshape(sequence_length, key_span_width)
    value_terms = value_terms.reshape(sequence_length, key_span_width)
    key_gradient, grad_value = (
        lax.psum_scatter(
            key_terms.astype(jnp.bfloat16), "zero", scatter_dimension=0, tiled=True
        ).astype(jnp.float32),
        lax.psum_scatter(
            value_terms.astype(jnp.bfloat16), "zero", scatter_dimension=0, tiled=True
        ).astype(jnp.float32),
    )
    grad_query = grad_query.reshape(token_rows, QUERY_HEADS, HEAD_SIZE) * score_scale
    key_gradient = key_gradient.reshape(token_rows, KEY_VALUE_HEADS, HEAD_SIZE)
    grad_query_normed = grad_query * cosine + rotate_back(grad_query * sine)
    grad_key_normed = key_gradient * cosine + rotate_back(key_gradient * sine)
    grad_query_gain = jnp.sum(grad_query_normed * query * query_scale, axis=(0, 1))
    grad_key_gain = jnp.sum(grad_key_normed * key * key_scale, axis=(0, 1))
    grad_query_pre = rms_back(grad_query_normed * query_gain, query, query_scale)
    grad_key_pre = rms_back(grad_key_normed * key_gain, key, key_scale)
    grad_projected = jnp.concatenate(
        [
            grad_query_pre.reshape(token_rows, query_span_width),
            grad_key_pre.reshape(token_rows, key_span_width),
            grad_value,
        ],
        axis=-1,
    ).astype(jnp.bfloat16)
    grad_qkv = jnp.einsum(
        "td,tf->df", normed_input, grad_projected, preferred_element_type=jnp.float32
    )
    grad_normed_input = jnp.einsum(
        "tf,df->td", grad_projected, qkv_weight, preferred_element_type=jnp.float32
    )
    grad_gain_one = jnp.sum(grad_normed_input * inputs * scale_one, axis=0)
    grad_input = grad_middle + rms_back(grad_normed_input * gain_one, inputs, scale_one)
    grad_norms = jnp.stack([grad_gain_one, grad_gain_two], axis=1)
    grad_heads = jnp.stack([grad_query_gain, grad_key_gain], axis=1)
    summed = (
        lax.psum_scatter(grad_qkv, ("dp", "zero"), scatter_dimension=0, tiled=True),
        lax.psum_scatter(grad_out, ("dp", "zero"), scatter_dimension=0, tiled=True),
        lax.psum_scatter(grad_gateup, ("dp", "zero"), scatter_dimension=0, tiled=True),
        lax.psum_scatter(grad_down, ("dp", "zero"), scatter_dimension=0, tiled=True),
        lax.psum_scatter(grad_norms, ("dp", "zero"), scatter_dimension=0, tiled=True),
        lax.psum_scatter(grad_heads, ("dp", "zero"), scatter_dimension=0, tiled=True),
    )
    updated = [
        adam_update(masters[index], summed[index], means[index], squares[index])
        for index in range(6)
    ]
    return (
        output[None],
        grad_input[None],
        summed[0],
        summed[1],
        summed[2],
        summed[3],
        summed[4],
        summed[5],
        updated[0][0],
        updated[1][0],
        updated[2][0],
        updated[3][0],
        updated[4][0],
        updated[5][0],
        updated[0][1],
        updated[1][1],
        updated[2][1],
        updated[3][1],
        updated[4][1],
        updated[5][1],
        updated[0][2],
        updated[1][2],
        updated[2][2],
        updated[3][2],
        updated[4][2],
        updated[5][2],
    )

def row_sum(value):
    return jnp.sum(value, axis=1)


def flip(axis, size, bits):
    return [(place, place ^ bits) for place in range(size)]


def gather_rows(block, axis, size):
    kept = [block] + [
        lax.ppermute(block, axis, flip(axis, size, bits)) for bits in range(2, size, 2)
    ]
    same_core = jnp.concatenate(kept, axis=0)
    other_core = lax.ppermute(same_core, axis, flip(axis, size, 1))
    return same_core, other_core


def scatter_rows(same_core, other_core, axis, size):
    arrived = lax.ppermute(other_core.astype(jnp.bfloat16), axis, flip(axis, size, 1))
    rows = same_core.shape[0] // (size // 2)
    pair = same_core + arrived.astype(jnp.float32)
    own = pair[:rows]
    sent = pair[rows:].astype(jnp.bfloat16)
    for place, bits in enumerate(range(2, size, 2)):
        piece = lax.ppermute(
            sent[place * rows : (place + 1) * rows], axis, flip(axis, size, bits)
        )
        own = own + piece.astype(jnp.float32)
    return own


def dot_nt(left, right):
    return lax.dot_general(
        left, right, (((1,), (1,)), ((), ())), preferred_element_type=jnp.float32
    )


def dot_tn(left, right):
    return lax.dot_general(
        left, right, (((0,), (0,)), ((), ())), preferred_element_type=jnp.float32
    )


def dot_nn(left, right):
    return jnp.dot(left, right, preferred_element_type=jnp.float32)


def build_split(dp_size, zero_size):
    copies = zero_size // KEY_VALUE_HEADS
    per_dp = KEY_VALUE_HEADS // dp_size if KEY_VALUE_HEADS % dp_size == 0 else 0
    regroup = copies == 1 and per_dp > 0
    local_heads = QUERY_HEADS // zero_size
    query_width = local_heads * HEAD_SIZE
    local_width = query_width + 2 * HEAD_SIZE
    query_span = QUERY_HEADS * HEAD_SIZE
    key_span = KEY_VALUE_HEADS * HEAD_SIZE
    score_scale = HEAD_SIZE ** (-0.5)
    places = [place for place in range(0, zero_size, 2)] + [
        place for place in range(1, zero_size, 2)
    ]

    def spread_heads(rows, width):
        count = rows.shape[0]
        if regroup:
            parts = rows.reshape(count, dp_size, per_dp, width)
            return jnp.transpose(parts, (2, 1, 0, 3)).reshape(zero_size, count, width)
        return jnp.transpose(rows.reshape(count, zero_size, width), (1, 0, 2))

    def join_heads(parts):
        count, width = parts.shape[1:]
        if regroup:
            split = parts.reshape(per_dp, dp_size, count, width)
            return jnp.transpose(split, (2, 1, 0, 3)).reshape(count, zero_size * width)
        return jnp.transpose(parts, (1, 0, 2)).reshape(count, zero_size * width)

    def spread_qkv(rows):
        query = spread_heads(rows[:, :query_span], query_width)
        key = rows[:, query_span : query_span + key_span]
        value = rows[:, query_span + key_span :]
        if copies > 1:
            key, value = [
                jnp.repeat(part.reshape(-1, KEY_VALUE_HEADS, HEAD_SIZE), copies, axis=1).reshape(
                    rows.shape[0], -1
                )
                for part in (key, value)
            ]
        return jnp.concatenate(
            [query, spread_heads(key, HEAD_SIZE), spread_heads(value, HEAD_SIZE)], axis=-1
        )

    def join_qkv(parts):
        query = join_heads(parts[..., :query_width])
        key, value = [
            join_heads(parts[..., start : start + HEAD_SIZE])
            for start in (query_width, query_width + HEAD_SIZE)
        ]
        if copies > 1:
            key, value = [
                part.reshape(-1, KEY_VALUE_HEADS, copies, HEAD_SIZE)
                .sum(axis=2)
                .reshape(query.shape[0], key_span)
                for part in (key, value)
            ]
        return jnp.concatenate([query, key, value], axis=-1)

    def spread_units(rows):
        count = rows.shape[0]
        units = FF // (dp_size * zero_size)
        parts = rows.reshape(count, 2, dp_size, zero_size, units)
        return jnp.transpose(parts, (3, 0, 1, 2, 4)).reshape(zero_size, count, 2 * FF // zero_size)

    def join_units(parts):
        count = parts.shape[1]
        units = FF // (dp_size * zero_size)
        split = parts.reshape(zero_size, count, 2, dp_size, units)
        return jnp.transpose(split, (1, 2, 3, 0, 4)).reshape(count, 2 * FF)

    groups = None
    if regroup:
        groups = [
            [part * dp_size + place for place in range(dp_size)] for part in range(per_dp)
        ]

    def gather_out(rows):
        if regroup:
            by_dp = lax.all_gather(rows, "dp", axis=0, tiled=False)
            mine = lax.all_to_all(by_dp, "zero", 0, 0, axis_index_groups=groups, tiled=True)
            return mine.reshape(query_width, rows.shape[1])
        every = lax.all_gather(rows, ("dp", "zero"), axis=0, tiled=True)
        return lax.dynamic_slice_in_dim(every, lax.axis_index("zero") * query_width, query_width)

    def scatter_out(grad):
        if regroup:
            parts = grad.reshape(dp_size, query_width // dp_size, grad.shape[1])
            by_dp = lax.all_to_all(parts, "zero", 0, 0, axis_index_groups=groups, tiled=True)
            return lax.psum_scatter(by_dp, "dp", scatter_dimension=0, tiled=False)
        every = jnp.zeros((query_span, grad.shape[1]), grad.dtype)
        every = lax.dynamic_update_slice_in_dim(
            every, grad, lax.axis_index("zero") * query_width, 0
        )
        return lax.psum_scatter(every, ("dp", "zero"), scatter_dimension=0, tiled=True)

    def on_device_split(
        block_input,
        out_cotangent,
        segment_ids,
        query_key_value_weight,
        w_out,
        w_gateup,
        w_down,
        norm_gains,
        head_gains,
        first_moment_projection,
        mean_out,
        mean_gateup,
        mean_down,
        mean_norms,
        mean_heads,
        second_moment_projection,
        square_out,
        square_gateup,
        square_down,
        square_norms,
        square_heads,
    ):
        masters = (query_key_value_weight, w_out, w_gateup, w_down, norm_gains, head_gains)
        means = (first_moment_projection, mean_out, mean_gateup, mean_down, mean_norms, mean_heads)
        squares = (
            second_moment_projection,
            square_out,
            square_gateup,
            square_down,
            square_norms,
            square_heads,
        )
        inputs = block_input[0]
        cotangent = out_cotangent[0]
        segments = segment_ids[0]
        token_rows = inputs.shape[0]
        sequence_length = segments.shape[0]
        half_length = sequence_length // 2
        width = inputs.shape[1]
        weight_rows = query_key_value_weight.shape[0]
        head_rows = head_gains.shape[0]
        low = lambda value: value.astype(jnp.bfloat16)
        wide = lambda value: value.astype(jnp.float32)
        place = lax.axis_index("zero")

        gains = wide(low(norm_gains))
        low_qkv = wide(low(query_key_value_weight))
        low_gateup = wide(low(w_gateup))
        scaled_qkv = low(low_qkv * gains[:, 0:1])
        scaled_gateup = low(low_gateup * gains[:, 1:2])
        small = jnp.zeros((weight_rows, HEAD_SIZE), jnp.bfloat16)
        small = lax.dynamic_update_slice(small, low(head_gains), (0, 0))
        small = jnp.broadcast_to(small[None], (zero_size, weight_rows, HEAD_SIZE))
        outgoing = jnp.concatenate(
            [spread_qkv(scaled_qkv), spread_units(scaled_gateup), small], axis=-1
        )
        incoming = lax.all_to_all(outgoing, "zero", 0, 0, tiled=True)
        group_rows = zero_size * weight_rows
        head_part = incoming[:, :head_rows, local_width + 2 * FF // zero_size :][..., :2]
        head_part = head_part.reshape(1, zero_size * head_rows * 2)
        head_part = jnp.pad(head_part, ((0, 15), (0, local_width - head_part.shape[1])))
        qkv_part = incoming[..., :local_width].reshape(group_rows, local_width)
        gateup_part = incoming[..., local_width : local_width + 2 * FF // zero_size].reshape(
            group_rows, 2 * FF // zero_size
        )
        qkv_every = lax.all_gather(
            jnp.concatenate([qkv_part, head_part], axis=0), "dp", axis=0, tiled=False
        )
        qkv_weight = qkv_every[:, :group_rows].reshape(width, local_width)
        heads = qkv_every[:, group_rows, : zero_size * head_rows * 2].reshape(HEAD_SIZE, 2)
        out_weight = gather_out(low(w_out))
        gateup_weight = lax.all_gather(gateup_part, "dp", axis=0, tiled=True)
        down_weight = lax.all_gather(low(w_down), "dp", axis=0, tiled=True)
        query_gain = wide(heads[:, 0])
        key_gain = wide(heads[:, 1])

        scale_one = rms_scale(inputs)
        unit_one = inputs * scale_one
        one_same, one_other = gather_rows(low(unit_one), "zero", zero_size)
        unit_full = jnp.concatenate([one_same, one_other], axis=0)
        cot_same, cot_other = gather_rows(low(cotangent), "zero", zero_size)
        cot_full = jnp.concatenate([cot_same, cot_other], axis=0)

        blocks = jnp.bitwise_xor(place, jnp.array(places, jnp.int32))
        positions = (
            blocks[:, None] * token_rows + jnp.arange(token_rows, dtype=jnp.int32)[None, :]
        ).reshape(sequence_length)
        ordered = jnp.take(segments.reshape(zero_size, token_rows), blocks, axis=0).reshape(
            sequence_length
        )
        cosine, sine = rope_tables(positions, HEAD_SIZE)
        allowed = (ordered[:, None] == ordered[None, :]) & (
            positions[:, None] >= positions[None, :]
        )

        projected = dot_nn(unit_full, qkv_weight)
        query = projected[:, :query_width].reshape(sequence_length, local_heads, HEAD_SIZE)
        key = projected[:, query_width : query_width + HEAD_SIZE]
        value_low = low(projected[:, query_width + HEAD_SIZE :])
        query_scale = rms_scale(query)
        key_scale = rms_scale(key)
        query_normed = query * query_scale * query_gain
        key_normed = key * key_scale * key_gain
        query_turned = low(
            query_normed * cosine[:, None, :] + rotate_half(query_normed) * sine[:, None, :]
        )
        key_turned = low(key_normed * cosine + rotate_half(key_normed) * sine)

        softs, lows, outs = [], [], []
        for head in range(local_heads):
            scores = dot_nt(query_turned[:, head], key_turned) * score_scale
            scores = jnp.where(allowed, scores, score_masked)
            top = jnp.max(scores, axis=-1, keepdims=True)
            weights = jnp.where(allowed, jnp.exp(scores - top), 0.0)
            soft = weights / jnp.sum(weights, axis=-1, keepdims=True)
            soft_low = low(soft)
            softs.append(soft)
            lows.append(soft_low)
            outs.append(low(dot_nn(soft_low, value_low)))
        attended = jnp.concatenate(outs, axis=-1)

        attended_same, attended_other = attended[:half_length], attended[half_length:]
        middle = inputs + scatter_rows(
            dot_nn(attended_same, out_weight), dot_nn(attended_other, out_weight), "zero", zero_size
        )
        scale_two = rms_scale(middle)
        unit_two = middle * scale_two
        two_same, two_other = gather_rows(low(unit_two), "zero", zero_size)
        two_full = jnp.concatenate([two_same, two_other], axis=0)
        gateup = dot_nn(two_full, gateup_weight)
        units = FF // zero_size
        gate = gateup[:, :units]
        upward = gateup[:, units:]
        sigma = jax.nn.sigmoid(gate)
        hidden = low(gate * sigma * upward)
        output = middle + scatter_rows(
            dot_nn(hidden[:half_length], down_weight),
            dot_nn(hidden[half_length:], down_weight),
            "zero",
            zero_size,
        )
        grad_hidden = dot_nt(cot_full, down_weight)
        gate_term = grad_hidden * upward * sigma * (1.0 + gate * (1.0 - sigma))
        up_term = grad_hidden * gate * sigma
        gateup_grad = low(jnp.concatenate([gate_term, up_term], axis=-1))
        scaled_grad = scatter_rows(
            dot_nt(gateup_grad[:half_length], gateup_weight),
            dot_nt(gateup_grad[half_length:], gateup_weight),
            "zero",
            zero_size,
        )
        down_sum = lax.psum_scatter(
            low(dot_tn(hidden, cot_full)), "dp", scatter_dimension=0, tiled=True
        )
        gateup_sum = lax.psum_scatter(
            low(dot_tn(two_full, gateup_grad)), "dp", scatter_dimension=0, tiled=True
        )
        grad_middle = cotangent + rms_back(scaled_grad, middle, scale_two)
        low_same, low_other = gather_rows(low(grad_middle), "zero", zero_size)
        middle_low = jnp.concatenate([low_same, low_other], axis=0)
        attended_grad = low(dot_nt(middle_low, out_weight))
        out_sum = scatter_out(low(dot_tn(attended, middle_low)))

        query_grads = []
        key_grad = jnp.zeros((sequence_length, HEAD_SIZE), jnp.float32)
        value_grad = jnp.zeros((sequence_length, HEAD_SIZE), jnp.float32)
        for head in range(local_heads):
            span = slice(head * HEAD_SIZE, (head + 1) * HEAD_SIZE)
            grad_out_head = attended_grad[:, span]
            delta = jnp.sum(wide(grad_out_head) * wide(outs[head]), axis=-1, keepdims=True)
            grad_soft = dot_nt(grad_out_head, value_low)
            grad_scores = low(softs[head] * (grad_soft - delta))
            query_grads.append(dot_nn(grad_scores, key_turned) * score_scale)
            key_grad = key_grad + dot_tn(grad_scores, query_turned[:, head]) * score_scale
            value_grad = value_grad + dot_tn(lows[head], grad_out_head)
        grad_query = jnp.stack(query_grads, axis=1)
        query_back = grad_query * cosine[:, None, :] + rotate_back(grad_query * sine[:, None, :])
        key_back = key_grad * cosine + rotate_back(key_grad * sine)
        gain_query = jnp.sum(query_back * query * query_scale, axis=(0, 1))
        gain_key = jnp.sum(key_back * key * key_scale, axis=0)
        query_pre = rms_back(query_back * query_gain, query, query_scale)
        key_pre = rms_back(key_back * key_gain, key, key_scale)
        grad_projected = low(
            jnp.concatenate(
                [query_pre.reshape(sequence_length, query_width), key_pre, value_grad], axis=-1
            )
        )
        qkv_partial = low(dot_tn(unit_full, grad_projected)).reshape(
            dp_size, group_rows, local_width
        )
        head_partial = low(jnp.stack([gain_query, gain_key], axis=1)).reshape(dp_size, 1, -1)
        head_partial = jnp.pad(
            head_partial, ((0, 0), (0, 15), (0, local_width - head_partial.shape[2]))
        )
        qkv_sum = lax.psum_scatter(
            jnp.concatenate([qkv_partial, head_partial], axis=1),
            "dp",
            scatter_dimension=0,
            tiled=False,
        )
        input_part = scatter_rows(
            dot_nt(grad_projected[:half_length], qkv_weight),
            dot_nt(grad_projected[half_length:], qkv_weight),
            "zero",
            zero_size,
        )
        grad_input = grad_middle + rms_back(input_part, inputs, scale_one)

        head_back = qkv_sum[group_rows, : zero_size * head_rows * 2].reshape(
            zero_size, head_rows, 2
        )
        head_back = jnp.pad(
            head_back, ((0, 0), (0, weight_rows - head_rows), (0, HEAD_SIZE - 2))
        )
        returned = lax.all_to_all(
            jnp.concatenate(
                [
                    qkv_sum[:group_rows].reshape(zero_size, weight_rows, local_width),
                    gateup_sum.reshape(zero_size, weight_rows, 2 * FF // zero_size),
                    head_back,
                ],
                axis=-1,
            ),
            "zero",
            0,
            0,
            tiled=True,
        )
        bare_qkv = join_qkv(wide(returned[..., :local_width]))
        bare_gateup = join_units(
            wide(returned[..., local_width : local_width + 2 * FF // zero_size])
        )
        grad_heads = jnp.sum(
            wide(returned[:, :head_rows, local_width + 2 * FF // zero_size :][..., :2]), axis=0
        )
        grad_norms = jnp.stack(
            [row_sum(low_qkv * bare_qkv), row_sum(low_gateup * bare_gateup)], axis=1
        )
        summed = (
            bare_qkv * gains[:, 0:1],
            wide(out_sum),
            bare_gateup * gains[:, 1:2],
            wide(down_sum),
            grad_norms,
            grad_heads,
        )
        updated = [
            adam_update(masters[index], summed[index], means[index], squares[index])
            for index in range(6)
        ]
        return (
            output[None],
            grad_input[None],
            *summed,
            *[update[0] for update in updated],
            *[update[1] for update in updated],
            *[update[2] for update in updated],
        )

    return on_device_split


def can_split(dp_size, zero_size):
    return (
        zero_size >= 2
        and zero_size & (zero_size - 1) == 0
        and zero_size % KEY_VALUE_HEADS == 0
        and QUERY_HEADS % zero_size == 0
        and FF % (dp_size * zero_size) == 0
    )


def solution(mesh):
    placed = (
        P("dp", "zero", None),
        P("dp", "zero", None),
        P("dp", None),
        P(("dp", "zero"), None),
        P(("dp", "zero"), None),
        P(("dp", "zero"), None),
        P(("dp", "zero"), None),
        P(("dp", "zero"), None),
        P(("dp", "zero"), None),
        P(("dp", "zero"), None),
        P(("dp", "zero"), None),
        P(("dp", "zero"), None),
        P(("dp", "zero"), None),
        P(("dp", "zero"), None),
        P(("dp", "zero"), None),
        P(("dp", "zero"), None),
        P(("dp", "zero"), None),
        P(("dp", "zero"), None),
        P(("dp", "zero"), None),
        P(("dp", "zero"), None),
        P(("dp", "zero"), None),
    )
    sizes = (mesh.shape["dp"], mesh.shape["zero"])
    body = build_split(*sizes) if can_split(*sizes) else on_device_gathered
    return jax.shard_map(
        body,
        mesh=mesh,
        in_specs=placed,
        out_specs=(
            P("dp", "zero", None),
            P("dp", "zero", None),
            P(("dp", "zero"), None),
            P(("dp", "zero"), None),
            P(("dp", "zero"), None),
            P(("dp", "zero"), None),
            P(("dp", "zero"), None),
            P(("dp", "zero"), None),
            P(("dp", "zero"), None),
            P(("dp", "zero"), None),
            P(("dp", "zero"), None),
            P(("dp", "zero"), None),
            P(("dp", "zero"), None),
            P(("dp", "zero"), None),
            P(("dp", "zero"), None),
            P(("dp", "zero"), None),
            P(("dp", "zero"), None),
            P(("dp", "zero"), None),
            P(("dp", "zero"), None),
            P(("dp", "zero"), None),
            P(("dp", "zero"), None),
            P(("dp", "zero"), None),
            P(("dp", "zero"), None),
            P(("dp", "zero"), None),
            P(("dp", "zero"), None),
            P(("dp", "zero"), None),
        ),
        check_vma=False,
    )
```
